32 devices in a mesh: con: 16 (over z, y, x), rep: 2 (over core).
Axes of the slice: x: 2, y: 2, z: 4, core: 2. Of those that a mesh axis runs over, the one named last changes fastest.
Arguments:
- tamps: bfloat16 [16384, 14336], P('rep', 'con'), may hold values from -6 to 6
- integrals: bfloat16 [1024, 16384], P('con', 'rep'), may hold values from -0.0625 to 0.0625
Outputs:
- ladder: bfloat16 [1024, 14336], P('rep', 'con')
The draws below stay inside these ranges and needn't reach their ends.
All inputs are finite; a program needn't handle non-finite values.
Results may differ from the reference program's by a relative error of at most 0.001.
Values may be sent and summed in bfloat16 or wider, within the bound.
A program may use at most 128 MiB of HBM per device.

```python
import jax
import jax.numpy as jnp
from jax import lax

CD = 16384
AB = 1024
OO = 14336


def raised(drawn, stream_key, source, target, parts, factor):
    def block_of(dim):
        return (jnp.arange(drawn.shape[dim]) // (drawn.shape[dim] // parts)).reshape((-1,) + (1,) * (drawn.ndim - 1 - dim))

    near = jax.random.permutation(stream_key, parts)[block_of(target)]
    far = (block_of(target) + parts // 2) % parts
    return jnp.where((block_of(source) == near) | (block_of(source) == far), factor * drawn, drawn)


def block_levels(own_key, extent, pieces, smallest, top_value):
    gain = 1.0
    for dim, blocks in pieces:
        draws = jax.random.uniform(jax.random.fold_in(jax.random.fold_in(own_key, 6), dim), (blocks,), jnp.float32, smallest / len(pieces), top_value / len(pieces))
        gain = gain * jnp.repeat(jnp.exp(draws), extent[dim] // blocks).reshape((-1,) + (1,) * (len(extent) - 1 - dim))
    return gain


def noise(rng, dims, deviation, most, shards=(), kind=jnp.bfloat16):
    entries = deviation * jax.random.normal(rng, dims, jnp.float32)
    if shards:
        entries = entries * block_levels(rng, dims, shards, -0.22, 0.18)
    return jnp.clip(entries, -most, most).astype(kind)


def bell_draw_with(own_key, shape, spread, bound, cuts, heavy, dtype=jnp.bfloat16):
    drawn = spread * jax.random.normal(own_key, shape, jnp.float32)
    if cuts:
        drawn = drawn * block_levels(own_key, shape, cuts, -0.22, 0.18)
    return jnp.clip(raised(drawn, jax.random.fold_in(own_key, 3), *heavy), -bound, bound).astype(dtype)


def setup_inputs(seed: int = 0) -> dict:
    arg_keys = jax.random.split(jax.random.key(seed), 3)
    return {
        "tamps": noise(arg_keys[0], (CD, OO), 1.0, 6.0, ((0, 2), (1, 16))),
        "integrals": bell_draw_with(arg_keys[1], (AB, CD), CD ** -0.5, 0.0625, ((0, 16), (1, 2)), (1, 0, 16, 2.0)),
    }


def reference(tamps, integrals):
    left = integrals.astype(jnp.float32)
    total = tamps.shape[1]
    width = 1024
    count = total // width
    if total % width != 0:
        width = total
        count = 1
    blocks = jnp.transpose(tamps.reshape(tamps.shape[0], count, width), (1, 0, 2))

    def one_block(piece):
        return jnp.dot(left, piece.astype(jnp.float32), preferred_element_type=jnp.float32)

    contracted = lax.map(one_block, blocks)
    contracted = jnp.transpose(contracted, (1, 0, 2)).reshape(integrals.shape[0], total)
    return contracted.astype(jnp.bfloat16)
```

```python
import functools

import jax
import jax.numpy as jnp
from jax import lax
from jax.experimental import pallas as pl
from jax.experimental.pallas import tpu as pltpu
from jax.sharding import PartitionSpec as P

MESH = pl.DeviceIdType.MESH
CHUNKS = 8
SLOTS = 40
LAG = 2
X, Y, UP, DOWN = range(4)


def plane_at(z, i):
    near = z + 1 - 2 * (z % 2)
    second = jnp.where(z < 2, 2, 1)
    third = jnp.where(z < 2, 3, 0)
    return jnp.where(i == 0, near, jnp.where(i == 1, second, third))


def message(way, t, x, y, z):
    own = y * 2 + x
    diagonal = (1 - y) * 2 + (1 - x)
    if way in (X, Y):
        side = (1 - y) * 2 + x if way == X else y * 2 + (1 - x)
        i = (t - 12) // 8
        q = t - 36
        if way == X:
            last_i = jnp.where(q == 0, 0, jnp.where(q == 3, 2, 1))
            last_c = jnp.where(q == 0, 6, jnp.where(q == 1, 5, jnp.where(q == 2, 7, 6)))
            ok = jnp.logical_or(t != 37, jnp.logical_or(z == 0, z == 3))
        else:
            last_i = jnp.where(q == 0, 0, jnp.where(q == 1, 1, 2))
            last_c = jnp.where(q == 0, 7, jnp.where(q == 1, 6, jnp.where(q == 2, 5, 7)))
            ok = t >= 0
        column = jnp.where(t < 8, own, jnp.where(t < 12, side, jnp.where(t < 36, own, side)))
        plane = jnp.where(t < 12, z, jnp.where(t < 36, plane_at(z, i), plane_at(z, last_i)))
        chunk = jnp.where(
            t < 8, t, jnp.where(t < 12, 2 * (t - 8) + way, jnp.where(t < 36, (t - 12) % 8, last_c))
        )
        return column, plane, chunk, ok
    far = jnp.where(t < 24, t // 8, jnp.where(t < 30, 0, jnp.where(t < 35, 1, 2)))
    chunk = jnp.where(t < 24, t % 8, jnp.where(t < 30, t - 24, jnp.where(t < 35, t - 30, t - 35)))
    column = jnp.where(t < 24, own, diagonal)
    if way == UP:
        plane = z - far
        ok = jnp.logical_and(jnp.logical_and(z >= 0, z < 3), plane >= 0)
    else:
        plane = z + far
        ok = jnp.logical_and(jnp.logical_and(z <= 3, z > 0), plane <= 3)
    return column, plane, chunk, ok


def units_ready(s):
    early = jnp.clip(s - 15, 0, 8) + 2 * jnp.clip(s - 27, 0, 8)
    late = jnp.clip(s - 34, 0, 4) + jnp.where(s >= 38, 1, 0) + jnp.where(s >= 39, 3, 0)
    return early + late


def kernel(
    tamps_hbm, slab_hbm, out_ref, held, amps, total, other,
    send_sem, recv_sem, own_sem, amps_sem, part_send, part_recv,
):
    me = lax.axis_index("con")
    core = lax.axis_index("rep")
    z, y, x = me // 4, (me // 2) % 2, me % 2
    rows = slab_hbm.shape[0]
    wide = slab_hbm.shape[1] // CHUNKS
    half = 2 * rows
    columns = amps.shape[1]
    own = y * 2 + x

    def device(x, y, z):
        return z * 4 + y * 2 + x

    def place(column, plane, chunk):
        start = pl.multiple_of((column * 4 + plane) * rows, rows)
        return held.at[chunk, pl.ds(start, rows), :]

    load_amps = pltpu.make_async_copy(tamps_hbm, amps, amps_sem)
    loads = [
        pltpu.make_async_copy(
            slab_hbm.at[:, pl.ds(c * wide, wide)], place(own, z, c), own_sem.at[c]
        )
        for c in range(CHUNKS)
    ]
    for load in loads:
        load.start()

    barrier = pltpu.get_barrier_semaphore()
    side = (device(1 - x, y, z), device(x, 1 - y, z))
    for to in side:
        pl.semaphore_signal(barrier, inc=1, device_id=(to, core), device_id_type=MESH)
    pl.semaphore_signal(barrier, inc=1, device_id=(me, 1 - core), device_id_type=MESH)

    @pl.when(z > 0)
    def _():
        pl.semaphore_signal(barrier, inc=1, device_id=(me - 4, core), device_id_type=MESH)

    @pl.when(z < 3)
    def _():
        pl.semaphore_signal(barrier, inc=1, device_id=(me + 4, core), device_id_type=MESH)

    ends = jnp.logical_or(z == 0, z == 3)
    pl.semaphore_wait(barrier, jnp.where(ends, 4, 5))

    for load in loads:
        load.wait()

    targets = (side[0], side[1], me + 4, me - 4)
    sources = ((1 - x, y, z), (x, 1 - y, z), (x, y, z - 1), (x, y, z + 1))

    def copy(way, t, piece):
        return pltpu.make_async_remote_copy(
            src_ref=piece,
            dst_ref=piece,
            send_sem=send_sem.at[way, t],
            recv_sem=recv_sem.at[way, t],
            device_id=(targets[way], core),
            device_id_type=MESH,
        )

    def send(t):
        for way in range(4):
            column, plane, chunk, ok = message(way, t, x, y, z)

            @pl.when(ok)
            def _():
                copy(way, t, place(column, plane, chunk)).start()

    def arrive(t):
        for way in range(4):
            column, plane, chunk, ok = message(way, t, *sources[way])

            @pl.when(ok)
            def _():
                copy(way, t, place(column, plane, chunk)).wait_recv()

    def product(u):
        m = u - 24
        pair = u - 8
        column = jnp.where(
            u < 8,
            own,
            jnp.where(
                u < 24,
                jnp.where(pair % 2 == 0, y * 2 + 1 - x, (1 - y) * 2 + x),
                (1 - y) * 2 + 1 - x,
            ),
        )
        late = jnp.where(m == 4, 5, jnp.where(m == 5, 4, m))
        chunk = jnp.where(u < 8, u, jnp.where(u < 24, pair // 2, late))
        left = held[chunk, pl.ds(pl.multiple_of(column * 4 * rows, 4 * rows), 4 * rows), :]
        deep = pl.ds(pl.multiple_of(chunk * wide, wide), wide)
        for first in range(0, columns, 256):
            cut = slice(first, min(first + 256, columns))
            total[column, :, cut] += jnp.dot(
                left, amps[deep, cut], preferred_element_type=jnp.float32
            )

    def hand_over(column):
        return pltpu.make_async_remote_copy(
            src_ref=total.at[column, pl.ds(pl.multiple_of((1 - core) * half, half), half), :],
            dst_ref=other.at[column],
            send_sem=part_send.at[column],
            recv_sem=part_recv.at[column],
            device_id=(me, 1 - core),
            device_id_type=MESH,
        )

    def step(t, _):
        @pl.when(t >= LAG)
        def _():
            arrive(t - LAG)

        @pl.when(t < SLOTS)
        def _():
            send(t)

        @pl.when(t == 8)
        def _():
            load_amps.start()
            total[...] = jnp.zeros_like(total)

        @pl.when(t == 16)
        def _():
            load_amps.wait()

        def unit(u, _):
            product(u)
            return 0

        lax.fori_loop(units_ready(t - LAG - 1), units_ready(t - LAG), unit, 0)

        @pl.when(t == 35 + LAG)
        def _():
            for column in (own, y * 2 + 1 - x, (1 - y) * 2 + x):
                hand_over(column).start()

        return 0

    lax.fori_loop(0, SLOTS + LAG, step, 0)
    hand_over((1 - y) * 2 + 1 - x).start()

    def drain(t, _):
        for way in range(4):
            column, plane, chunk, ok = message(way, t, x, y, z)

            @pl.when(ok)
            def _():
                copy(way, t, place(column, plane, chunk)).wait_send()

        return 0

    lax.fori_loop(0, SLOTS, drain, 0)

    def finish(column):
        hand_over(column).wait()
        mine = total[column, pl.ds(pl.multiple_of(core * half, half), half), :] + other[column]
        for k in range(2):
            start = pl.multiple_of((k * 4 + column) * rows, rows)
            out_ref[pl.ds(start, rows), :] = mine[k * rows : (k + 1) * rows].astype(out_ref.dtype)

    for column in (own, y * 2 + 1 - x, (1 - y) * 2 + x, (1 - y) * 2 + 1 - x):
        finish(column)


def linked(tamps, integrals):
    rows, depth = integrals.shape
    columns = tamps.shape[1]
    return pl.pallas_call(
        kernel,
        out_shape=jax.ShapeDtypeStruct((8 * rows, columns), jnp.bfloat16),
        in_specs=[pl.BlockSpec(memory_space=pl.ANY)] * 2,
        out_specs=pl.BlockSpec(memory_space=pltpu.VMEM),
        scratch_shapes=[
            pltpu.VMEM((CHUNKS, 16 * rows, depth // CHUNKS), jnp.bfloat16),
            pltpu.VMEM((depth, columns), jnp.bfloat16),
            pltpu.VMEM((4, 4 * rows, columns), jnp.float32),
            pltpu.VMEM((4, 2 * rows, columns), jnp.float32),
            pltpu.SemaphoreType.DMA((4, SLOTS)),
            pltpu.SemaphoreType.DMA((4, SLOTS)),
            pltpu.SemaphoreType.DMA((CHUNKS,)),
            pltpu.SemaphoreType.DMA,
            pltpu.SemaphoreType.DMA((4,)),
            pltpu.SemaphoreType.DMA((4,)),
        ],
        compiler_params=pltpu.CompilerParams(
            collective_id=0, has_side_effects=True, vmem_limit_bytes=56 * 2**20
        ),
    )(tamps, integrals)


def shards(tamps, integrals):
    gathered = lax.all_gather(integrals, "con", axis=0, tiled=True)
    partial_value = jnp.dot(gathered, tamps, preferred_element_type=jnp.float32)
    summed = lax.psum_scatter(partial_value, "rep", scatter_dimension=0, tiled=True)
    return summed.astype(jnp.bfloat16)


def solution(mesh):
    in_specs = (P("rep", "con"), P("con", "rep"))
    out_specs = P("rep", "con")
    part = linked if (mesh.shape["con"], mesh.shape["rep"]) == (16, 2) else shards
    return jax.shard_map(part, mesh=mesh, in_specs=in_specs, out_specs=out_specs, check_vma=False)
```

```python
import functools

import jax
import jax.numpy as jnp
from jax import lax
from jax.experimental import pallas as pl
from jax.experimental.pallas import tpu as pltpu
from jax.sharding import PartitionSpec as P

MESH = pl.DeviceIdType.MESH
CHUNKS = 8
SLOTS = 40
LAG = 4
X, Y, UP, DOWN = range(4)


def plane_at(z, i):
    near = z + 1 - 2 * (z % 2)
    second = jnp.where(z < 2, 2, 1)
    third = jnp.where(z < 2, 3, 0)
    return jnp.where(i == 0, near, jnp.where(i == 1, second, third))


def turned(n):
    return jnp.where(n < 16, n, n + 5) % 8


def message(way, t, x, y, z):
    own = y * 2 + x
    diagonal = (1 - y) * 2 + (1 - x)
    if way in (X, Y):
        side = (1 - y) * 2 + x if way == X else y * 2 + (1 - x)
        i = (t - 12) // 8
        q = t - 36
        if way == X:
            last_i = jnp.where(q == 1, 0, 1)
            last_c = jnp.where(q == 0, 6, jnp.where(q == 3, 4, 7))
        else:
            last_i = jnp.where(q == 3, 0, 2)
            last_c = jnp.where(q == 3, 4, 5 + q)
        column = jnp.where(t < 8, own, jnp.where(t < 12, side, jnp.where(t < 36, own, side)))
        plane = jnp.where(t < 12, z, jnp.where(t < 36, plane_at(z, i), plane_at(z, last_i)))
        chunk = jnp.where(
            t < 8, t, jnp.where(t < 12, 2 * (t - 8) + way, jnp.where(t < 36, turned(t - 12), last_c))
        )
        ends = jnp.logical_or(z == 0, z == 3)
        ok = t >= 0 if way == X else jnp.logical_or(t != 39, ends)
        return column, plane, chunk, ok
    extra = jnp.logical_and(t == 30, z == (0 if way == UP else 3))
    far = jnp.where(t < 24, t // 8, jnp.where(t < 30, 0, jnp.where(t < 35, 1, 2)))
    far = jnp.where(extra, 0, far)
    k = jnp.where(t < 30, t - 24, (t - 30) % 5)
    column = jnp.where(t < 24, own, diagonal)
    if way == UP:
        plane = z - far
        ok = jnp.logical_and(jnp.logical_and(z >= 0, z < 3), plane >= 0)
        i = jnp.where(z == 1, far + 1, far)
    else:
        plane = z + far
        ok = jnp.logical_and(jnp.logical_and(z <= 3, z > 0), plane <= 3)
        i = jnp.where(z == 2, far + 1, far)
    fifth = jnp.where(i == 2, 4, 5)
    chunk = jnp.where(t < 24, t % 8, jnp.where(k < 4, k, jnp.where(k == 4, fifth, 6)))
    chunk = jnp.where(extra, 4, chunk)
    ok = jnp.logical_and(ok, jnp.logical_or(t != 29, i == 0))
    return column, plane, chunk, ok


def units_ready(s):
    early = jnp.clip(s - 15, 0, 8) + 2 * jnp.clip(s - 27, 0, 8)
    late = jnp.clip(s - 34, 0, 1) + 2 * jnp.clip(s - 35, 0, 3)
    return early + late


def kernel(
    tamps_hbm, slab_hbm, out_ref, held, amps, total, other,
    send_sem, recv_sem, own_sem, amps_sem, part_send, part_recv,
):
    me = lax.axis_index("con")
    core = lax.axis_index("rep")
    z, y, x = me // 4, (me // 2) % 2, me % 2
    rows = slab_hbm.shape[0]
    wide = slab_hbm.shape[1] // CHUNKS
    half = 2 * rows
    columns = amps.shape[1]
    own = y * 2 + x

    def device(x, y, z):
        return z * 4 + y * 2 + x

    def place(column, plane, chunk):
        start = pl.multiple_of((column * 4 + plane) * rows, rows)
        return held.at[chunk, pl.ds(start, rows), :]

    load_amps = pltpu.make_async_copy(tamps_hbm, amps, amps_sem)

    def load(c):
        cut = pl.ds(pl.multiple_of(c * wide, wide), wide)
        return pltpu.make_async_copy(slab_hbm.at[:, cut], place(own, z, c), own_sem.at[c])

    for c in range(CHUNKS):
        load(c).start()

    barrier = pltpu.get_barrier_semaphore()
    side = (device(1 - x, y, z), device(x, 1 - y, z))
    for to in side:
        pl.semaphore_signal(barrier, inc=1, device_id=(to, core), device_id_type=MESH)
    pl.semaphore_signal(barrier, inc=1, device_id=(me, 1 - core), device_id_type=MESH)

    @pl.when(z > 0)
    def _():
        pl.semaphore_signal(barrier, inc=1, device_id=(me - 4, core), device_id_type=MESH)

    @pl.when(z < 3)
    def _():
        pl.semaphore_signal(barrier, inc=1, device_id=(me + 4, core), device_id_type=MESH)

    ends = jnp.logical_or(z == 0, z == 3)
    pl.semaphore_wait(barrier, jnp.where(ends, 4, 5))

    targets = (side[0], side[1], me + 4, me - 4)
    sources = ((1 - x, y, z), (x, 1 - y, z), (x, y, z - 1), (x, y, z + 1))

    def copy(way, t, piece):
        return pltpu.make_async_remote_copy(
            src_ref=piece,
            dst_ref=piece,
            send_sem=send_sem.at[way, t],
            recv_sem=recv_sem.at[way, t],
            device_id=(targets[way], core),
            device_id_type=MESH,
        )

    def send(t):
        for way in range(4):
            column, plane, chunk, ok = message(way, t, x, y, z)

            @pl.when(ok)
            def _():
                copy(way, t, place(column, plane, chunk)).start()

    def arrive(t):
        for way in range(4):
            column, plane, chunk, ok = message(way, t, *sources[way])

            @pl.when(ok)
            def _():
                copy(way, t, place(column, plane, chunk)).wait_recv()

    def sent(t):
        for way in range(4):
            column, plane, chunk, ok = message(way, t, x, y, z)

            @pl.when(ok)
            def _():
                copy(way, t, place(column, plane, chunk)).wait_send()

    def product(u):
        m = u - 24
        pair = u - 8
        column = jnp.where(
            u < 8,
            own,
            jnp.where(
                u < 24,
                jnp.where(pair % 2 == 0, y * 2 + 1 - x, (1 - y) * 2 + x),
                (1 - y) * 2 + 1 - x,
            ),
        )
        late = jnp.where(m % 2 == 1, (m + 1) // 2, jnp.where(m == 0, 0, 4 + m // 2))
        chunk = jnp.where(u < 8, u, jnp.where(u < 24, (pair // 2 + 5) % 8, late))
        multiply(column, chunk, 0, 4 * rows)

    def multiply(column, chunk, first_row, count):
        start = pl.multiple_of(column * 4 * rows + first_row, count)
        left = held[chunk, pl.ds(start, count), :]
        deep = pl.ds(pl.multiple_of(chunk * wide, wide), wide)
        into = pl.ds(pl.multiple_of(first_row, count), count)
        for first in range(0, columns, 256):
            cut = slice(first, min(first + 256, columns))
            total[column, into, cut] += jnp.dot(
                left, amps[deep, cut], preferred_element_type=jnp.float32
            )

    def hand_over(column):
        return pltpu.make_async_remote_copy(
            src_ref=total.at[column, pl.ds(pl.multiple_of((1 - core) * half, half), half), :],
            dst_ref=other.at[column],
            send_sem=part_send.at[column],
            recv_sem=part_recv.at[column],
            device_id=(me, 1 - core),
            device_id_type=MESH,
        )

    def finish(column):
        hand_over(column).wait()
        mine = total[column, pl.ds(pl.multiple_of(core * half, half), half), :] + other[column]
        for k in range(2):
            start = pl.multiple_of((k * 4 + column) * rows, rows)
            out_ref[pl.ds(start, rows), :] = mine[k * rows : (k + 1) * rows].astype(out_ref.dtype)

    def step(t, _):
        @pl.when(t >= LAG)
        def _():
            arrive(t - LAG)

        @pl.when(t < CHUNKS)
        def _():
            load(t).wait()

        @pl.when(t < SLOTS)
        def _():
            send(t)

        @pl.when(t >= LAG)
        def _():
            sent(t - LAG)

        @pl.when(t == 8)
        def _():
            load_amps.start()
            total[...] = jnp.zeros_like(total)

        @pl.when(t == 16)
        def _():
            load_amps.wait()

        def unit(u, _):
            product(u)
            return 0

        lax.fori_loop(units_ready(t - LAG - 1), units_ready(t - LAG), unit, 0)

        @pl.when(t == 35 + LAG)
        def _():
            for column in (own, y * 2 + 1 - x, (1 - y) * 2 + x):
                hand_over(column).start()

        @pl.when(t == SLOTS + LAG - 2)
        def _():
            for column in (own, y * 2 + 1 - x, (1 - y) * 2 + x):
                finish(column)

        return 0

    lax.fori_loop(0, SLOTS + LAG, step, 0)
    diagonal = (1 - y) * 2 + 1 - x
    multiply(diagonal, 4, (1 - core) * half, half)
    hand_over(diagonal).start()
    multiply(diagonal, 4, core * half, half)

    finish(diagonal)


def linked(tamps, integrals):
    rows, depth = integrals.shape
    columns = tamps.shape[1]
    return pl.pallas_call(
        kernel,
        out_shape=pltpu.VMEM((8 * rows, columns), jnp.bfloat16),
        in_specs=[pl.BlockSpec(memory_space=pl.ANY)] * 2,
        out_specs=pl.BlockSpec(memory_space=pltpu.VMEM),
        scratch_shapes=[
            pltpu.VMEM((CHUNKS, 16 * rows, depth // CHUNKS), jnp.bfloat16),
            pltpu.VMEM((depth, columns), jnp.bfloat16),
            pltpu.VMEM((4, 4 * rows, columns), jnp.float32),
            pltpu.VMEM((4, 2 * rows, columns), jnp.float32),
            pltpu.SemaphoreType.DMA((4, SLOTS)),
            pltpu.SemaphoreType.DMA((4, SLOTS)),
            pltpu.SemaphoreType.DMA((CHUNKS,)),
            pltpu.SemaphoreType.DMA,
            pltpu.SemaphoreType.DMA((4,)),
            pltpu.SemaphoreType.DMA((4,)),
        ],
        compiler_params=pltpu.CompilerParams(
            collective_id=0, has_side_effects=True, vmem_limit_bytes=56 * 2**20
        ),
    )(tamps, integrals)


def shards(tamps, integrals):
    gathered = lax.all_gather(integrals, "con", axis=0, tiled=True)
    partial_value = jnp.dot(gathered, tamps, preferred_element_type=jnp.float32)
    summed = lax.psum_scatter(partial_value, "rep", scatter_dimension=0, tiled=True)
    return summed.astype(jnp.bfloat16)


def solution(mesh):
    in_specs = (P("rep", "con"), P("con", "rep"))
    out_specs = P("rep", "con")
    part = linked if (mesh.shape["con"], mesh.shape["rep"]) == (16, 2) else shards
    return jax.shard_map(part, mesh=mesh, in_specs=in_specs, out_specs=out_specs, check_vma=False)
```

```python
import functools

import jax
import jax.numpy as jnp
from jax import lax
from jax.experimental import pallas as pl
from jax.experimental.pallas import tpu as pltpu
from jax.sharding import PartitionSpec as P

MESH = pl.DeviceIdType.MESH
CHUNKS = 8
SLOTS = 40
LAG = 4
X, Y, UP, DOWN = range(4)


def plane_at(z, i):
    near = z + 1 - 2 * (z % 2)
    second = jnp.where(z < 2, 2, 1)
    third = jnp.where(z < 2, 3, 0)
    return jnp.where(i == 0, near, jnp.where(i == 1, second, third))


def turned(n):
    return jnp.where(n < 16, n, n + 5) % 8


def message(way, t, x, y, z):
    own = y * 2 + x
    diagonal = (1 - y) * 2 + (1 - x)
    if way in (X, Y):
        side = (1 - y) * 2 + x if way == X else y * 2 + (1 - x)
        i = (t - 12) // 8
        q = t - 36
        if way == X:
            last_i = jnp.where(q == 1, 0, 1)
            last_c = jnp.where(q == 0, 6, jnp.where(q == 3, 4, 7))
        else:
            last_i = jnp.where(q == 3, 0, 2)
            last_c = jnp.where(q == 3, 4, 5 + q)
        column = jnp.where(t < 8, own, jnp.where(t < 12, side, jnp.where(t < 36, own, side)))
        plane = jnp.where(t < 12, z, jnp.where(t < 36, plane_at(z, i), plane_at(z, last_i)))
        chunk = jnp.where(
            t < 8, t, jnp.where(t < 12, 2 * (t - 8) + way, jnp.where(t < 36, turned(t - 12), last_c))
        )
        ends = jnp.logical_or(z == 0, z == 3)
        ok = t >= 0 if way == X else jnp.logical_or(t != 39, ends)
        return column, plane, chunk, ok
    extra = jnp.logical_and(t == 30, z == (0 if way == UP else 3))
    far = jnp.where(t < 24, t // 8, jnp.where(t < 30, 0, jnp.where(t < 35, 1, 2)))
    far = jnp.where(extra, 0, far)
    k = jnp.where(t < 30, t - 24, (t - 30) % 5)
    column = jnp.where(t < 24, own, diagonal)
    if way == UP:
        plane = z - far
        ok = jnp.logical_and(jnp.logical_and(z >= 0, z < 3), plane >= 0)
        i = jnp.where(z == 1, far + 1, far)
    else:
        plane = z + far
        ok = jnp.logical_and(jnp.logical_and(z <= 3, z > 0), plane <= 3)
        i = jnp.where(z == 2, far + 1, far)
    fifth = jnp.where(i == 2, 4, 5)
    chunk = jnp.where(t < 24, t % 8, jnp.where(k < 4, k, jnp.where(k == 4, fifth, 6)))
    chunk = jnp.where(extra, 4, chunk)
    ok = jnp.logical_and(ok, jnp.logical_or(t != 29, i == 0))
    return column, plane, chunk, ok


def units_ready(s):
    early = jnp.clip(s - 15, 0, 8) + 2 * jnp.clip(s - 27, 0, 8)
    late = jnp.clip(s - 34, 0, 1) + 2 * jnp.clip(s - 35, 0, 3)
    return early + late


def kernel(
    tamps_hbm, slab_hbm, out_ref, held, amps, total, other,
    send_sem, recv_sem, own_sem, amps_sem, part_send, part_recv,
):
    me = lax.axis_index("con")
    core = lax.axis_index("rep")
    z, y, x = me // 4, (me // 2) % 2, me % 2
    rows = slab_hbm.shape[0]
    wide = slab_hbm.shape[1] // CHUNKS
    half = 2 * rows
    columns = amps.shape[1]
    own = y * 2 + x

    def device(x, y, z):
        return z * 4 + y * 2 + x

    def place(column, plane, chunk):
        start = pl.multiple_of((column * 4 + plane) * rows, rows)
        return held.at[chunk, pl.ds(start, rows), :]

    load_amps = pltpu.make_async_copy(tamps_hbm, amps, amps_sem)

    def load(c):
        cut = pl.ds(pl.multiple_of(c * wide, wide), wide)
        return pltpu.make_async_copy(slab_hbm.at[:, cut], place(own, z, c), own_sem.at[c])

    barrier = pltpu.get_barrier_semaphore()
    side = (device(1 - x, y, z), device(x, 1 - y, z))
    for to in side:
        pl.semaphore_signal(barrier, inc=1, device_id=(to, core), device_id_type=MESH)
    pl.semaphore_signal(barrier, inc=1, device_id=(me, 1 - core), device_id_type=MESH)

    @pl.when(z > 0)
    def _():
        pl.semaphore_signal(barrier, inc=1, device_id=(me - 4, core), device_id_type=MESH)

    @pl.when(z < 3)
    def _():
        pl.semaphore_signal(barrier, inc=1, device_id=(me + 4, core), device_id_type=MESH)

    for c in range(CHUNKS):
        load(c).start()

    ends = jnp.logical_or(z == 0, z == 3)
    pl.semaphore_wait(barrier, jnp.where(ends, 4, 5))

    targets = (side[0], side[1], me + 4, me - 4)
    sources = ((1 - x, y, z), (x, 1 - y, z), (x, y, z - 1), (x, y, z + 1))

    def copy(way, t, piece):
        return pltpu.make_async_remote_copy(
            src_ref=piece,
            dst_ref=piece,
            send_sem=send_sem.at[way, t],
            recv_sem=recv_sem.at[way, t],
            device_id=(targets[way], core),
            device_id_type=MESH,
        )

    def send(t):
        for way in range(4):
            column, plane, chunk, ok = message(way, t, x, y, z)

            @pl.when(ok)
            def _():
                copy(way, t, place(column, plane, chunk)).start()

    def arrive(t):
        for way in range(4):
            column, plane, chunk, ok = message(way, t, *sources[way])

            @pl.when(ok)
            def _():
                copy(way, t, place(column, plane, chunk)).wait_recv()

    def sent(t):
        for way in range(4):
            column, plane, chunk, ok = message(way, t, x, y, z)

            @pl.when(ok)
            def _():
                copy(way, t, place(column, plane, chunk)).wait_send()

    def product(u):
        m = u - 24
        pair = u - 8
        column = jnp.where(
            u < 8,
            own,
            jnp.where(
                u < 24,
                jnp.where(pair % 2 == 0, y * 2 + 1 - x, (1 - y) * 2 + x),
                (1 - y) * 2 + 1 - x,
            ),
        )
        late = jnp.where(m % 2 == 1, (m + 1) // 2, jnp.where(m == 0, 0, 4 + m // 2))
        chunk = jnp.where(u < 8, u, jnp.where(u < 24, (pair // 2 + 5) % 8, late))
        multiply(column, chunk, 0, 4 * rows)

    def multiply(column, chunk, first_row, count):
        start = pl.multiple_of(column * 4 * rows + first_row, count)
        left = held[chunk, pl.ds(start, count), :]
        deep = pl.ds(pl.multiple_of(chunk * wide, wide), wide)
        into = pl.ds(pl.multiple_of(first_row, count), count)
        for first in range(0, columns, 256):
            cut = slice(first, min(first + 256, columns))
            total[column, into, cut] += jnp.dot(
                left, amps[deep, cut], preferred_element_type=jnp.float32
            )

    def hand_over(column):
        return pltpu.make_async_remote_copy(
            src_ref=total.at[column, pl.ds(pl.multiple_of((1 - core) * half, half), half), :],
            dst_ref=other.at[column],
            send_sem=part_send.at[column],
            recv_sem=part_recv.at[column],
            device_id=(me, 1 - core),
            device_id_type=MESH,
        )

    def finish(column):
        hand_over(column).wait()
        mine = total[column, pl.ds(pl.multiple_of(core * half, half), half), :] + other[column]
        for k in range(2):
            start = pl.multiple_of((k * 4 + column) * rows, rows)
            out_ref[pl.ds(start, rows), :] = mine[k * rows : (k + 1) * rows].astype(out_ref.dtype)

    def step(t, _):
        @pl.when(t >= LAG)
        def _():
            arrive(t - LAG)

        @pl.when(t < CHUNKS)
        def _():
            load(t).wait()

        @pl.when(t < SLOTS)
        def _():
            send(t)

        @pl.when(t >= LAG)
        def _():
            sent(t - LAG)

        @pl.when(t == 8)
        def _():
            load_amps.start()
            total[...] = jnp.zeros_like(total)

        @pl.when(t == 16)
        def _():
            load_amps.wait()

        def unit(u, _):
            product(u)
            return 0

        lax.fori_loop(units_ready(t - LAG - 1), units_ready(t - LAG), unit, 0)

        @pl.when(t == 35 + LAG)
        def _():
            for column in (own, y * 2 + 1 - x, (1 - y) * 2 + x):
                hand_over(column).start()

        return 0

    lax.fori_loop(0, SLOTS + LAG, step, 0)
    diagonal = (1 - y) * 2 + 1 - x
    multiply(diagonal, 4, (1 - core) * half, half)
    hand_over(diagonal).start()
    multiply(diagonal, 4, core * half, half)

    for column in (own, y * 2 + 1 - x, (1 - y) * 2 + x, diagonal):
        finish(column)


def linked(tamps, integrals):
    rows, depth = integrals.shape
    columns = tamps.shape[1]
    return pl.pallas_call(
        kernel,
        out_shape=pltpu.VMEM((8 * rows, columns), jnp.bfloat16),
        in_specs=[pl.BlockSpec(memory_space=pl.ANY)] * 2,
        out_specs=pl.BlockSpec(memory_space=pltpu.VMEM),
        scratch_shapes=[
            pltpu.VMEM((CHUNKS, 16 * rows, depth // CHUNKS), jnp.bfloat16),
            pltpu.VMEM((depth, columns), jnp.bfloat16),
            pltpu.VMEM((4, 4 * rows, columns), jnp.float32),
            pltpu.VMEM((4, 2 * rows, columns), jnp.float32),
            pltpu.SemaphoreType.DMA((4, SLOTS)),
            pltpu.SemaphoreType.DMA((4, SLOTS)),
            pltpu.SemaphoreType.DMA((CHUNKS,)),
            pltpu.SemaphoreType.DMA,
            pltpu.SemaphoreType.DMA((4,)),
            pltpu.SemaphoreType.DMA((4,)),
        ],
        compiler_params=pltpu.CompilerParams(
            collective_id=0, has_side_effects=True, vmem_limit_bytes=56 * 2**20
        ),
    )(tamps, integrals)


def shards(tamps, integrals):
    gathered = lax.all_gather(integrals, "con", axis=0, tiled=True)
    partial_value = jnp.dot(gathered, tamps, preferred_element_type=jnp.float32)
    summed = lax.psum_scatter(partial_value, "rep", scatter_dimension=0, tiled=True)
    return summed.astype(jnp.bfloat16)


def solution(mesh):
    in_specs = (P("rep", "con"), P("con", "rep"))
    out_specs = P("rep", "con")
    part = linked if (mesh.shape["con"], mesh.shape["rep"]) == (16, 2) else shards
    return jax.shard_map(part, mesh=mesh, in_specs=in_specs, out_specs=out_specs, check_vma=False)
```

```python
import functools

import jax
import jax.numpy as jnp
from jax import lax
from jax.experimental import pallas as pl
from jax.experimental.pallas import tpu as pltpu
from jax.sharding import PartitionSpec as P

MESH = pl.DeviceIdType.MESH
CHUNKS = 8
SLOTS = 40
LAG = 4
X, Y, UP, DOWN = range(4)


def plane_at(z, i):
    near = z + 1 - 2 * (z % 2)
    second = jnp.where(z < 2, 2, 1)
    third = jnp.where(z < 2, 3, 0)
    return jnp.where(i == 0, near, jnp.where(i == 1, second, third))


def turned(n):
    return jnp.where(n < 16, n, n + 5) % 8


def message(way, t, x, y, z):
    own = y * 2 + x
    diagonal = (1 - y) * 2 + (1 - x)
    if way in (X, Y):
        side = (1 - y) * 2 + x if way == X else y * 2 + (1 - x)
        i = (t - 12) // 8
        q = t - 36
        if way == X:
            last_i = jnp.where(q == 1, 0, 1)
            last_c = jnp.where(q == 0, 6, jnp.where(q == 3, 4, 7))
        else:
            last_i = jnp.where(q == 3, 0, 2)
            last_c = jnp.where(q == 3, 4, 5 + q)
        column = jnp.where(t < 8, own, jnp.where(t < 12, side, jnp.where(t < 36, own, side)))
        plane = jnp.where(t < 12, z, jnp.where(t < 36, plane_at(z, i), plane_at(z, last_i)))
        chunk = jnp.where(
            t < 8, t, jnp.where(t < 12, 2 * (t - 8) + way, jnp.where(t < 36, turned(t - 12), last_c))
        )
        ends = jnp.logical_or(z == 0, z == 3)
        ok = t >= 0 if way == X else jnp.logical_or(t != 39, ends)
        return column, plane, chunk, ok
    extra = jnp.logical_and(t == 30, z == (0 if way == UP else 3))
    far = jnp.where(t < 24, t // 8, jnp.where(t < 30, 0, jnp.where(t < 35, 1, 2)))
    far = jnp.where(extra, 0, far)
    k = jnp.where(t < 30, t - 24, (t - 30) % 5)
    column = jnp.where(t < 24, own, diagonal)
    if way == UP:
        plane = z - far
        ok = jnp.logical_and(jnp.logical_and(z >= 0, z < 3), plane >= 0)
        i = jnp.where(z == 1, far + 1, far)
    else:
        plane = z + far
        ok = jnp.logical_and(jnp.logical_and(z <= 3, z > 0), plane <= 3)
        i = jnp.where(z == 2, far + 1, far)
    fifth = jnp.where(i == 2, 4, 5)
    chunk = jnp.where(t < 24, t % 8, jnp.where(k < 4, k, jnp.where(k == 4, fifth, 6)))
    chunk = jnp.where(extra, 4, chunk)
    ok = jnp.logical_and(ok, jnp.logical_or(t != 29, i == 0))
    return column, plane, chunk, ok


def units_ready(s):
    early = jnp.clip(s - 15, 0, 8) + 2 * jnp.clip(s - 27, 0, 8)
    late = jnp.clip(s - 34, 0, 1) + 2 * jnp.clip(s - 35, 0, 3)
    return early + late


def kernel(
    tamps_hbm, slab_hbm, out_ref, held, amps, total, other,
    send_sem, recv_sem, own_sem, amps_sem, part_send, part_recv,
):
    me = lax.axis_index("con")
    core = lax.axis_index("rep")
    z, y, x = me // 4, (me // 2) % 2, me % 2
    rows = slab_hbm.shape[0]
    wide = slab_hbm.shape[1] // CHUNKS
    half = 2 * rows
    columns = amps.shape[1]
    own = y * 2 + x

    def device(x, y, z):
        return z * 4 + y * 2 + x

    def place(column, plane, chunk):
        start = pl.multiple_of((column * 4 + plane) * rows, rows)
        return held.at[chunk, pl.ds(start, rows), :]

    load_amps = pltpu.make_async_copy(tamps_hbm, amps, amps_sem)

    def load(c):
        cut = pl.ds(pl.multiple_of(c * wide, wide), wide)
        return pltpu.make_async_copy(slab_hbm.at[:, cut], place(own, z, c), own_sem.at[c])

    barrier = pltpu.get_barrier_semaphore()
    side = (device(1 - x, y, z), device(x, 1 - y, z))
    for to in side:
        pl.semaphore_signal(barrier, inc=1, device_id=(to, core), device_id_type=MESH)
    pl.semaphore_signal(barrier, inc=1, device_id=(me, 1 - core), device_id_type=MESH)

    @pl.when(z > 0)
    def _():
        pl.semaphore_signal(barrier, inc=1, device_id=(me - 4, core), device_id_type=MESH)

    @pl.when(z < 3)
    def _():
        pl.semaphore_signal(barrier, inc=1, device_id=(me + 4, core), device_id_type=MESH)

    for c in range(CHUNKS):
        load(c).start()

    ends = jnp.logical_or(z == 0, z == 3)
    pl.semaphore_wait(barrier, jnp.where(ends, 4, 5))

    targets = (side[0], side[1], me + 4, me - 4)
    sources = ((1 - x, y, z), (x, 1 - y, z), (x, y, z - 1), (x, y, z + 1))

    def copy(way, t, piece):
        return pltpu.make_async_remote_copy(
            src_ref=piece,
            dst_ref=piece,
            send_sem=send_sem.at[way, t],
            recv_sem=recv_sem.at[way, t],
            device_id=(targets[way], core),
            device_id_type=MESH,
        )

    def send(t):
        for way in (UP, DOWN, X, Y):
            column, plane, chunk, ok = message(way, t, x, y, z)

            @pl.when(ok)
            def _():
                copy(way, t, place(column, plane, chunk)).start()

    def arrive(t):
        for way in (UP, DOWN, X, Y):
            column, plane, chunk, ok = message(way, t, *sources[way])

            @pl.when(ok)
            def _():
                copy(way, t, place(column, plane, chunk)).wait_recv()

    def sent(t):
        for way in (UP, DOWN, X, Y):
            column, plane, chunk, ok = message(way, t, x, y, z)

            @pl.when(ok)
            def _():
                copy(way, t, place(column, plane, chunk)).wait_send()

    def product(u):
        m = u - 24
        pair = u - 8
        column = jnp.where(
            u < 8,
            own,
            jnp.where(
                u < 24,
                jnp.where(pair % 2 == 0, y * 2 + 1 - x, (1 - y) * 2 + x),
                (1 - y) * 2 + 1 - x,
            ),
        )
        late = jnp.where(m % 2 == 1, (m + 1) // 2, jnp.where(m == 0, 0, 4 + m // 2))
        chunk = jnp.where(u < 8, u, jnp.where(u < 24, (pair // 2 + 5) % 8, late))
        multiply(column, chunk, 0, 4 * rows)

    def multiply(column, chunk, first_row, count):
        start = pl.multiple_of(column * 4 * rows + first_row, count)
        left = held[chunk, pl.ds(start, count), :]
        deep = pl.ds(pl.multiple_of(chunk * wide, wide), wide)
        into = pl.ds(pl.multiple_of(first_row, count), count)
        for first in range(0, columns, 256):
            cut = slice(first, min(first + 256, columns))
            total[column, into, cut] += jnp.dot(
                left, amps[deep, cut], preferred_element_type=jnp.float32
            )

    def hand_over(column):
        return pltpu.make_async_remote_copy(
            src_ref=total.at[column, pl.ds(pl.multiple_of((1 - core) * half, half), half), :],
            dst_ref=other.at[column],
            send_sem=part_send.at[column],
            recv_sem=part_recv.at[column],
            device_id=(me, 1 - core),
            device_id_type=MESH,
        )

    def finish(column):
        hand_over(column).wait()
        mine = total[column, pl.ds(pl.multiple_of(core * half, half), half), :] + other[column]
        for k in range(2):
            start = pl.multiple_of((k * 4 + column) * rows, rows)
            out_ref[pl.ds(start, rows), :] = mine[k * rows : (k + 1) * rows].astype(out_ref.dtype)

    def step(t, _):
        @pl.when(t >= LAG)
        def _():
            arrive(t - LAG)

        @pl.when(t < CHUNKS)
        def _():
            load(t).wait()

        @pl.when(t < SLOTS)
        def _():
            send(t)

        @pl.when(t >= LAG)
        def _():
            sent(t - LAG)

        @pl.when(t == 8)
        def _():
            load_amps.start()
            total[...] = jnp.zeros_like(total)

        @pl.when(t == 16)
        def _():
            load_amps.wait()

        def unit(u, _):
            product(u)
            return 0

        lax.fori_loop(units_ready(t - LAG - 1), units_ready(t - LAG), unit, 0)

        @pl.when(t == 35 + LAG)
        def _():
            for column in (own, y * 2 + 1 - x, (1 - y) * 2 + x):
                hand_over(column).start()

        return 0

    lax.fori_loop(0, SLOTS + LAG, step, 0)
    diagonal = (1 - y) * 2 + 1 - x
    multiply(diagonal, 4, (1 - core) * half, half)
    hand_over(diagonal).start()
    multiply(diagonal, 4, core * half, half)

    for column in (own, y * 2 + 1 - x, (1 - y) * 2 + x, diagonal):
        finish(column)


def linked(tamps, integrals):
    rows, depth = integrals.shape
    columns = tamps.shape[1]
    return pl.pallas_call(
        kernel,
        out_shape=pltpu.VMEM((8 * rows, columns), jnp.bfloat16),
        in_specs=[pl.BlockSpec(memory_space=pl.ANY)] * 2,
        out_specs=pl.BlockSpec(memory_space=pltpu.VMEM),
        scratch_shapes=[
            pltpu.VMEM((CHUNKS, 16 * rows, depth // CHUNKS), jnp.bfloat16),
            pltpu.VMEM((depth, columns), jnp.bfloat16),
            pltpu.VMEM((4, 4 * rows, columns), jnp.float32),
            pltpu.VMEM((4, 2 * rows, columns), jnp.float32),
            pltpu.SemaphoreType.DMA((4, SLOTS)),
            pltpu.SemaphoreType.DMA((4, SLOTS)),
            pltpu.SemaphoreType.DMA((CHUNKS,)),
            pltpu.SemaphoreType.DMA,
            pltpu.SemaphoreType.DMA((4,)),
            pltpu.SemaphoreType.DMA((4,)),
        ],
        compiler_params=pltpu.CompilerParams(
            collective_id=0, has_side_effects=True, vmem_limit_bytes=56 * 2**20
        ),
    )(tamps, integrals)


def shards(tamps, integrals):
    gathered = lax.all_gather(integrals, "con", axis=0, tiled=True)
    partial_value = jnp.dot(gathered, tamps, preferred_element_type=jnp.float32)
    summed = lax.psum_scatter(partial_value, "rep", scatter_dimension=0, tiled=True)
    return summed.astype(jnp.bfloat16)


def solution(mesh):
    in_specs = (P("rep", "con"), P("con", "rep"))
    out_specs = P("rep", "con")
    part = linked if (mesh.shape["con"], mesh.shape["rep"]) == (16, 2) else shards
    return jax.shard_map(part, mesh=mesh, in_specs=in_specs, out_specs=out_specs, check_vma=False)
```
